1024 devices in a mesh: ctx: 128 (over z, x, core), kvh: 8 (over y).
Axes of the slice: x: 8, y: 8, z: 8, core: 2. Of those that a mesh axis runs over, the one named last changes fastest.
Arguments:
- queries: bfloat16 [16384, 8192], P('ctx', 'kvh'), may hold values from -6 to 6
- keys: bfloat16 [16384, 1024], P('ctx', 'kvh'), may hold values from -6 to 6
- values: bfloat16 [16384, 1024], P('ctx', 'kvh'), may hold values from -6 to 6
- upstream: bfloat16 [16384, 8192], P('ctx', 'kvh'), may hold values from -6 to 6
- selected: int32 [128, 8], P('ctx'), may hold values from -1 to 254, as said below
- counts: int32 [128], P('ctx'), may hold values from 1 to 8, as said below
Outputs:
- attention: bfloat16 [16384, 8192], P('ctx', 'kvh')
- grad_queries: bfloat16 [16384, 8192], P(('ctx', 'kvh'))
- grad_keys: float32 [16384, 1024], P('ctx', 'kvh')
- grad_values: float32 [16384, 1024], P('ctx', 'kvh')
The draws below stay inside these ranges and needn't reach their ends.
Inputs may be any that keep to these rules, and one draw needn't show every extreme that they name: `selected`: slot 0 of query block b is key block 2 b. Slot j >= 1 names one of the 2 key blocks held by the index of ctx that lies 2 ** (j - 1) below the index holding query block b, or is -1 where that index would be negative. counts[b] is at most 1 plus the number of non-negative remote slots of query block b; all slots j < counts[b] are non-negative.
All inputs are finite; a program needn't handle non-finite values.
Results may differ from the reference program's by a relative error of at most 0.04.
Values may be sent and summed in bfloat16 or wider, within the bound.
No kernel may reach another device: no remote copies, remote signals or barrier semaphores. Data moves between devices by JAX's collectives and lax.ppermute only.
A program may use at most 32 MiB of HBM per device.

```python
import math
import jax
import jax.numpy as jnp
from jax import lax

HD = 128
GROUP = 8
KVH = 8
KBLK = 64
QBLK = 128
SLOTS = 8
QB_DEV = 1
KB_DEV = 2
NQB = 128
TOKENS = 16384


def selection_tables(key):
    block_ids = jnp.arange(NQB, dtype=jnp.int32)
    owner_dev = block_ids // QB_DEV
    distances = jnp.left_shift(jnp.int32(1), jnp.arange(SLOTS - 1, dtype=jnp.int32))
    source_dev = owner_dev[:, None] - distances[None, :]
    usable = source_dev >= 0
    available = jnp.sum(usable.astype(jnp.int32), axis=1)
    raw_count = jax.random.randint(jax.random.fold_in(key, 11), (NQB,), 1, SLOTS + 1)
    live_count = jnp.minimum(raw_count, 1 + available)
    live_count = jnp.where(block_ids == NQB - 1, 1 + available, live_count).astype(jnp.int32)
    inner = jax.random.randint(jax.random.fold_in(key, 13), (NQB, SLOTS - 1), 0, KB_DEV)
    remote = jnp.where(usable, source_dev * KB_DEV + inner, -1).astype(jnp.int32)
    chosen = jnp.concatenate([(2 * block_ids)[:, None], remote], axis=1).astype(jnp.int32)
    return (chosen, live_count)


def draw_selected(key, part):
    return selection_tables(key)[0]


def draw_counts(key, part):
    return selection_tables(key)[1]


def draw_queries(key, part):
    shape = (TOKENS, KVH * GROUP * HD)
    bulk = jnp.clip(jax.random.normal(jax.random.fold_in(key, 41), shape, jnp.float32), -6.0, 6.0)
    return bulk.astype(jnp.bfloat16)


def draw_keys(key, part):
    shape = (TOKENS, KVH * HD)
    bulk = jnp.clip(jax.random.normal(jax.random.fold_in(key, 42), shape, jnp.float32), -6.0, 6.0)
    return bulk.astype(jnp.bfloat16)


def block_scale(stream_key, extent, cuts, low, largest):
    factor_of = 1.0
    for axis_at, blocks in cuts:
        draws = jax.random.uniform(jax.random.fold_in(jax.random.fold_in(stream_key, 6), axis_at), (blocks,), jnp.float32, low / len(cuts), largest / len(cuts))
        factor_of = factor_of * jnp.repeat(jnp.exp(draws), extent[axis_at] // blocks).reshape((-1,) + (1,) * (len(extent) - 1 - axis_at))
    return factor_of


def noise(stream_key, extent, scale, limit, pieces=(), held_as=jnp.bfloat16):
    result = scale * jax.random.normal(stream_key, extent, jnp.float32)
    if pieces:
        result = result * block_scale(stream_key, extent, pieces, -0.22, 0.18)
    return jnp.clip(result, -limit, limit).astype(held_as)


def setup_inputs(seed: int = 0) -> dict:
    streams_of = jax.random.split(jax.random.key(seed), 7)
    return {
        "queries": draw_queries(jax.random.fold_in(streams_of[6], 71), 0),
        "keys": draw_keys(jax.random.fold_in(streams_of[6], 71), 0),
        "values": noise(streams_of[2], (TOKENS, KVH * HD), 1.0, 6.0, ((0, 128), (1, 8))),
        "upstream": noise(streams_of[3], (TOKENS, KVH * GROUP * HD), 1.0, 6.0, ((0, 128), (1, 8))),
        "selected": draw_selected(jax.random.fold_in(streams_of[6], 71), 0),
        "counts": draw_counts(jax.random.fold_in(streams_of[6], 71), 0),
    }


def block_pass(query_heads, key_rows, value_rows, grad_heads, visible):
    score_scale = 1.0 / math.sqrt(HD)
    scores = jnp.einsum('ihd,sd->his', query_heads.astype(jnp.float32), key_rows.astype(jnp.float32)) * score_scale
    scores = jnp.where(visible[None], scores, jnp.float32(-1e+30))
    peak = lax.optimization_barrier(jnp.max(scores, axis=-1, keepdims=True))
    expon = jnp.exp(scores - peak)
    prob = expon / lax.optimization_barrier(jnp.sum(expon, axis=-1, keepdims=True))
    prob_half = prob.astype(jnp.bfloat16)
    attended = jnp.einsum('his,sd->ihd', prob_half.astype(jnp.float32), value_rows.astype(jnp.float32)).astype(jnp.bfloat16)
    grad_probs = jnp.einsum('ihd,sd->his', grad_heads.astype(jnp.float32), value_rows.astype(jnp.float32))
    row_term = lax.optimization_barrier(jnp.sum(grad_heads.astype(jnp.float32) * attended.astype(jnp.float32), axis=-1))
    grad_scores = (prob * (grad_probs - jnp.transpose(row_term)[:, :, None]) * score_scale).astype(jnp.bfloat16)
    grad_query = jnp.einsum('his,sd->ihd', grad_scores.astype(jnp.float32), key_rows.astype(jnp.float32)).astype(jnp.bfloat16)
    key_term = jnp.einsum('his,ihd->sd', grad_scores.astype(jnp.float32), query_heads.astype(jnp.float32))
    value_term = jnp.einsum('his,ihd->sd', prob_half.astype(jnp.float32), grad_heads.astype(jnp.float32))
    return (attended, grad_query, key_term, value_term)

def reference(queries, keys, values, upstream, selected, counts):
    width = GROUP * HD
    slot_index = jnp.arange(SLOTS * KBLK, dtype=jnp.int32) // KBLK
    offsets = jnp.arange(SLOTS * KBLK, dtype=jnp.int32) % KBLK

    def one_block(running, block_id):
        key_acc, value_acc = running
        first_row = (block_id * QBLK).astype(jnp.int32)
        query_rows = lax.dynamic_slice_in_dim(queries, first_row, QBLK, 0)
        grad_rows = lax.dynamic_slice_in_dim(upstream, first_row, QBLK, 0)
        chosen = selected[block_id]
        live_count = counts[block_id]
        key_pos = chosen[slot_index] * KBLK + offsets
        token_rows = jnp.clip(key_pos, 0, TOKENS - 1)
        query_pos = first_row + jnp.arange(QBLK, dtype=jnp.int32)
        visible = (slot_index < live_count)[None, :] & (key_pos[None, :] <= query_pos[:, None])
        outputs = []
        grads = []
        for group in range(KVH):
            query_heads = query_rows[:, group * width:(group + 1) * width].reshape(QBLK, GROUP, HD)
            grad_heads = grad_rows[:, group * width:(group + 1) * width].reshape(QBLK, GROUP, HD)
            key_rows = keys[token_rows, group * HD:(group + 1) * HD]
            value_rows = values[token_rows, group * HD:(group + 1) * HD]
            attended, grad_query, key_term, value_term = block_pass(query_heads, key_rows, value_rows, grad_heads, visible)
            outputs.append(attended.reshape(QBLK, width))
            grads.append(grad_query.reshape(QBLK, width))
            key_acc = key_acc.at[token_rows, group * HD:(group + 1) * HD].add(key_term)
            value_acc = value_acc.at[token_rows, group * HD:(group + 1) * HD].add(value_term)
        return ((key_acc, value_acc), (jnp.concatenate(outputs, axis=1), jnp.concatenate(grads, axis=1)))
    start_acc = (jnp.zeros((TOKENS, KVH * HD), jnp.float32), jnp.zeros((TOKENS, KVH * HD), jnp.float32))
    (key_acc, value_acc), (attn_blocks, grad_blocks) = lax.scan(one_block, start_acc, jnp.arange(NQB, dtype=jnp.int32))
    attention = attn_blocks.reshape(TOKENS, KVH * width)
    grad_queries = grad_blocks.reshape(TOKENS, KVH * width)
    return (attention, grad_queries, key_acc, value_acc)
```

```python
import math

import jax
import jax.numpy as jnp
from jax import lax
from jax.experimental import pallas as pl
from jax.experimental.pallas import tpu as pltpu
from jax.sharding import PartitionSpec as P

HD = 128
GROUP = 8
KBLK = 64
QBLK = 128
SLOTS = 8
PAIR = 2 * HD
KEYS = SLOTS * KBLK
TERM_ROWS = KBLK + 8
SCALE = 1.0 / math.sqrt(HD)
SCALE_LOG2 = SCALE * math.log2(math.e)
ORDER = (6, 3, 5, 2, 4, 1, 0)


VMEM = pl.BlockSpec(memory_space=pltpu.VMEM)
SMEM = pl.BlockSpec(memory_space=pltpu.SMEM)
ANY = pl.BlockSpec(memory_space=pl.ANY)


def from_behind(value, axis, steps):
    count = lax.axis_size(axis)
    initial, last = (max(0, -steps), min(count, count - steps))
    return lax.ppermute(value, axis, [(source, source + steps) for source in range(initial, last)])


def pack_kernel(k_ref, v_ref, o_ref, sems):
    first = pltpu.make_async_copy(k_ref, o_ref.at[pl.ds(0, QBLK)], sems.at[0])
    second = pltpu.make_async_copy(v_ref, o_ref.at[pl.ds(QBLK, QBLK)], sems.at[1])
    first.start()
    second.start()
    first.wait()
    second.wait()


def pack(keys, values):
    return pl.pallas_call(
        pack_kernel,
        out_shape=jax.ShapeDtypeStruct((2 * QBLK, HD), jnp.bfloat16),
        in_specs=[ANY, ANY],
        out_specs=VMEM,
        scratch_shapes=[pltpu.SemaphoreType.DMA((2,))],
        compiler_params=pltpu.CompilerParams(vmem_limit_bytes=1024 * 1024),
        cost_estimate=pl.CostEstimate(flops=0, bytes_accessed=4 * QBLK * HD * 2, transcendentals=0),
    )(keys, values)


def dot(a, b, contract):
    return lax.dot_general(a, b, (contract, ((), ())), preferred_element_type=jnp.float32)


def attend_kernel(sel_ref, cnt_ref, q_ref, u_ref, own_ref, *refs):
    near = refs[: SLOTS - 1]
    att_ref, dq_ref, own_out = refs[SLOTS - 1 : SLOTS + 2]
    terms = refs[SLOTS + 2 : 2 * SLOTS + 1]
    k_s, v_s, bias_s, kt_s, vt_s = refs[2 * SLOTS + 1 :]

    k_s[pl.ds(0, KBLK), :] = own_ref[pl.ds(0, KBLK), :]
    v_s[pl.ds(0, KBLK), :] = own_ref[pl.ds(QBLK, KBLK), :]
    key_at = lax.broadcasted_iota(jnp.int32, (KBLK, QBLK), 0)
    query_at = lax.broadcasted_iota(jnp.int32, (KBLK, QBLK), 1)
    bias_s[pl.ds(0, KBLK), :] = jnp.where(key_at <= query_at, 0.0, -1e30).astype(jnp.float32)
    for j in range(1, SLOTS):
        inner = sel_ref[0, j] & 1
        row = pl.multiple_of(inner * KBLK, KBLK)
        k_s[pl.ds(j * KBLK, KBLK), :] = near[j - 1][pl.ds(row, KBLK), :]
        v_s[pl.ds(j * KBLK, KBLK), :] = near[j - 1][pl.ds(QBLK + row, KBLK), :]
        dead = jnp.where(j < cnt_ref[0], 0.0, -1e30).astype(jnp.float32)
        bias_s[pl.ds(j * KBLK, KBLK), :] = jnp.full((KBLK, QBLK), dead, jnp.float32)
        terms[j - 1][pl.ds(KBLK, 8), :] = jnp.full((8, PAIR), inner.astype(jnp.float32)).astype(
            jnp.bfloat16
        )

    k = k_s[...]
    v = v_s[...]
    k_t = k.T
    v_t = v.T
    for pair in range(GROUP // 2):
        columns = [pl.ds((2 * pair + side) * HD, HD) for side in range(2)]
        q = jnp.concatenate([q_ref[:, c] for c in columns], axis=0)
        u = jnp.concatenate([u_ref[:, c] for c in columns], axis=0)
        bias = bias_s[...]
        bias = jnp.concatenate([bias, bias], axis=1)
        scores = dot(k, q, ((1,), (1,))) * SCALE_LOG2 + bias
        peak = jnp.max(scores, axis=0, keepdims=True)
        expon = jnp.exp2(scores - peak)
        prob = expon * (1.0 / jnp.sum(expon, axis=0, keepdims=True))
        half = prob.astype(jnp.bfloat16)
        grad_probs = dot(v, u, ((1,), (1,)))
        row_term = jnp.sum(prob * grad_probs, axis=0, keepdims=True)
        grad = (prob * (grad_probs - row_term)).astype(jnp.bfloat16)
        att = dot(v_t, half, ((1,), (0,)))
        dq = dot(k_t, grad, ((1,), (0,))) * SCALE
        for side in range(2):
            part = slice(side * QBLK, (side + 1) * QBLK)
            att_ref[:, columns[side]] = att[:, part].T.astype(jnp.bfloat16)
            dq_ref[:, columns[side]] = dq[:, part].T.astype(jnp.bfloat16)
        key_term = dot(grad, q, ((1,), (0,)))
        value_term = dot(half, u, ((1,), (0,)))
        if pair == 0:
            kt_s[...] = key_term
            vt_s[...] = value_term
        else:
            kt_s[...] += key_term
            vt_s[...] += value_term
    own_out[:, pl.ds(0, HD)] = kt_s[pl.ds(0, KBLK), :] * SCALE
    own_out[:, pl.ds(HD, HD)] = vt_s[pl.ds(0, KBLK), :]
    for j in range(1, SLOTS):
        rows = pl.ds(j * KBLK, KBLK)
        terms[j - 1][pl.ds(0, KBLK), pl.ds(0, HD)] = (kt_s[rows, :] * SCALE).astype(jnp.bfloat16)
        terms[j - 1][pl.ds(0, KBLK), pl.ds(HD, HD)] = vt_s[rows, :].astype(jnp.bfloat16)


def attend(selected, counts, queries, upstream, own, near):
    wide = jax.ShapeDtypeStruct((QBLK, GROUP * HD), jnp.bfloat16)
    term = jax.ShapeDtypeStruct((TERM_ROWS, PAIR), jnp.bfloat16)
    return pl.pallas_call(
        attend_kernel,
        out_shape=[wide, wide, jax.ShapeDtypeStruct((KBLK, PAIR), jnp.float32)]
        + [term] * (SLOTS - 1),
        in_specs=[SMEM, SMEM] + [VMEM] * (SLOTS + 2),
        out_specs=[VMEM] * (SLOTS + 2),
        scratch_shapes=[
            pltpu.VMEM((KEYS, HD), jnp.bfloat16),
            pltpu.VMEM((KEYS, HD), jnp.bfloat16),
            pltpu.VMEM((KEYS, QBLK), jnp.float32),
            pltpu.VMEM((KEYS, HD), jnp.float32),
            pltpu.VMEM((KEYS, HD), jnp.float32),
        ],
        compiler_params=pltpu.CompilerParams(vmem_limit_bytes=16 * 1024 * 1024),
        cost_estimate=pl.CostEstimate(
            flops=6 * 2 * GROUP * QBLK * KEYS * HD,
            bytes_accessed=2 * 1024 * 1024,
            transcendentals=GROUP * QBLK * KEYS,
        ),
    )(selected, counts, queries, upstream, own, *near)


def finish_kernel(dq_ref, own_ref, *refs):
    arrived = refs[: SLOTS - 1]
    gq_ref, gk_ref, gv_ref, sems = refs[SLOTS - 1 :]
    rows = QBLK // 8
    moves = [
        pltpu.make_async_copy(
            dq_ref.at[pl.ds(peer * rows, rows)],
            gq_ref.at[:, pl.ds(peer * GROUP * HD, GROUP * HD)],
            sems.at[peer],
        )
        for peer in range(8)
    ]
    for move in moves:
        move.start()
    low = own_ref[...]
    high = jnp.zeros((KBLK, PAIR), jnp.float32)
    for ref in arrived:
        value = ref[pl.ds(0, KBLK), :].astype(jnp.float32)
        inner = jnp.concatenate([ref[pl.ds(KBLK, 8), :].astype(jnp.float32)] * (KBLK // 8), axis=0)
        upper = value * inner
        high = high + upper
        low = low + (value - upper)
    gk_ref[pl.ds(0, KBLK), :] = low[:, :HD]
    gk_ref[pl.ds(KBLK, KBLK), :] = high[:, :HD]
    gv_ref[pl.ds(0, KBLK), :] = low[:, HD:]
    gv_ref[pl.ds(KBLK, KBLK), :] = high[:, HD:]
    for move in moves:
        move.wait()


def finish(dq, own, arrived):
    grad = jax.ShapeDtypeStruct((QBLK, HD), jnp.float32)
    return pl.pallas_call(
        finish_kernel,
        out_shape=[jax.ShapeDtypeStruct((QBLK // 8, 8 * GROUP * HD), jnp.bfloat16), grad, grad],
        in_specs=[VMEM] * (SLOTS + 1),
        out_specs=[ANY, VMEM, VMEM],
        scratch_shapes=[pltpu.SemaphoreType.DMA((8,))],
        compiler_params=pltpu.CompilerParams(vmem_limit_bytes=8 * 1024 * 1024),
        cost_estimate=pl.CostEstimate(flops=0, bytes_accessed=1024 * 1024, transcendentals=0),
    )(dq, own, *arrived)


def on_device(queries, keys, values, upstream, selected, counts):
    own = pack(keys, values)
    near = [None] * (SLOTS - 1)
    for j in ORDER:
        near[j] = from_behind(own, "ctx", 1 << j)
    attention, grad_query, own_term, *terms = attend(
        selected, counts, queries, upstream, own, near
    )
    arrived = [None] * (SLOTS - 1)
    for j in ORDER:
        arrived[j] = from_behind(terms[j], "ctx", -(1 << j))
    moved = lax.all_to_all(grad_query, "kvh", split_axis=0, concat_axis=0, tiled=True)
    grad_tokens, grad_keys, grad_values = finish(moved, own_term, arrived)
    return (attention, grad_tokens, grad_keys, grad_values)


def solution(mesh):
    placed = (
        P("ctx", "kvh"),
        P("ctx", "kvh"),
        P("ctx", "kvh"),
        P("ctx", "kvh"),
        P("ctx", None),
        P("ctx"),
    )
    return jax.shard_map(
        on_device,
        mesh=mesh,
        in_specs=placed,
        out_specs=(P("ctx", "kvh"), P(("ctx", "kvh"), None), P("ctx", "kvh"), P("ctx", "kvh")),
        check_vma=False,
    )
```
